32 devices in a mesh: ada: 4 (over y, core), avg: 8 (over z, x).
Axes of the slice: x: 2, y: 2, z: 4, core: 2. Of those that a mesh axis runs over, the one named last changes fastest.
Arguments:
- edges: float32 [49152, 1536], P(('ada', 'avg')), may hold values from -6 to 6
- teacher: float32 [49152, 512], P(('ada', 'avg')), may hold values from -9.5 to 9.5
- w_first: float32 [1536, 512], replicated, may hold values from -0.15625 to 0.15625
- b_first: float32 [512], replicated, may hold values from -3 to 3
- w_second: float32 [512, 512], replicated, may hold values from -0.25 to 0.25
- b_second: float32 [512], replicated, may hold values from -3 to 3
- norm_gain: float32 [512], replicated, may hold values from 0.5 to 1.5
- norm_shift: float32 [512], replicated, may hold values from -3 to 3
Outputs:
- new_w_first: float32 [1536, 512], replicated
- new_b_first: float32 [512], replicated
- new_w_second: float32 [512, 512], replicated
- new_b_second: float32 [512], replicated
- new_gain: float32 [512], replicated
- new_shift: float32 [512], replicated
The draws below stay inside these ranges and needn't reach their ends.
All inputs are finite; a program needn't handle non-finite values.
Results may differ from the reference program's by a relative error of at most 0.0003.
Values sent between devices are 32-bit elements; how exact they have to be, the bound alone decides.
A program may use at most 128 MiB of HBM per device.

```python
import jax
import jax.numpy as jnp
import numpy as np
from jax import lax

D_IN = 1536
D_HID = 512
ROWS = 1536
REPLICAS = 32
LEVELS = 2
N_ADA = 4
N_AVG = 8


def draw_teacher(key, part):
    noise_key = jax.random.fold_in(key, 11)
    block_key = jax.random.fold_in(key, 23)
    common_key = jax.random.fold_in(key, 37)
    noise = jnp.clip(jax.random.normal(noise_key, (ROWS * REPLICAS, D_HID), jnp.float32), -4.0, 4.0)
    own = jnp.clip(jax.random.normal(block_key, (REPLICAS, D_HID), jnp.float32), -2.5, 2.5)
    common = jnp.clip(jax.random.normal(common_key, (1, D_HID), jnp.float32), -2.5, 2.5)
    offsets = 1.5 * common + 0.6 * own
    spread_offsets = jnp.repeat(offsets, ROWS, axis=0)
    return (noise + spread_offsets).astype(jnp.float32)


def levels(own_key, extent, shards, smallest, largest):
    gain = 1.0
    for position, parts in shards:
        heights = jax.random.uniform(jax.random.fold_in(jax.random.fold_in(own_key, 6), position), (parts,), jnp.float32, smallest / len(shards), largest / len(shards))
        gain = gain * jnp.repeat(jnp.exp(heights), extent[position] // parts).reshape((-1,) + (1,) * (len(extent) - 1 - position))
    return gain


def normal_values(key, dims, width, reach, shards=(), kind=jnp.bfloat16):
    entries = width * jax.random.normal(key, dims, jnp.float32)
    if shards:
        entries = entries * levels(key, dims, shards, -0.22, 0.18)
    return jnp.clip(entries, -reach, reach).astype(kind)


def setup_inputs(seed: int = 0) -> dict:
    splits = jax.random.split(jax.random.key(seed), 9)
    edges = normal_values(splits[0], (ROWS * REPLICAS, D_IN), 1.0, 6.0, ((0, 32),), jnp.float32)
    teacher = draw_teacher(jax.random.fold_in(splits[8], 71), 0)
    w_first = normal_values(splits[2], (D_IN, D_HID), D_IN ** -0.5, 0.15625, (), jnp.float32)
    b_first = normal_values(splits[3], (D_HID,), 0.5, 3.0, (), jnp.float32)
    w_second = normal_values(splits[4], (D_HID, D_HID), D_HID ** -0.5, 0.25, (), jnp.float32)
    b_second = normal_values(splits[5], (D_HID,), 0.5, 3.0, (), jnp.float32)
    norm_gain = jnp.clip(1.0 + 0.1 * jax.random.normal(splits[6], (D_HID,), jnp.float32), 0.5, 1.5)
    norm_shift = normal_values(splits[7], (D_HID,), 0.5, 3.0, (), jnp.float32)
    return dict(edges=edges, teacher=teacher, w_first=w_first, b_first=b_first, w_second=w_second, b_second=b_second, norm_gain=norm_gain, norm_shift=norm_shift)


norm_eps = 1e-06
step_rate = 2.0
high = lax.Precision.HIGHEST

def local_loss(params, inputs, targets):
    w_first, b_first, w_second, b_second, norm_gain, norm_shift = params
    zfirst = jnp.dot(inputs, w_first, precision=high, preferred_element_type=jnp.float32) + b_first
    hidden = zfirst * jax.nn.sigmoid(zfirst)
    zsecond = jnp.dot(hidden, w_second, precision=high, preferred_element_type=jnp.float32) + b_second
    center = zsecond - lax.optimization_barrier(jnp.mean(zsecond, axis=1, keepdims=True))
    spread = lax.optimization_barrier(jnp.mean(center * center, axis=1, keepdims=True))
    output = center * lax.rsqrt(spread + 1e-05) * norm_gain + norm_shift
    return 0.5 * jnp.sum((output - targets) ** 2) / inputs.shape[0]

def reference(edges, teacher, w_first, b_first, w_second, b_second, norm_gain, norm_shift):
    params = (w_first, b_first, w_second, b_second, norm_gain, norm_shift)
    grad_fn = jax.grad(local_loss)

    def one_replica(index):
        start = (index * ROWS).astype(jnp.int32)
        inputs = lax.dynamic_slice_in_dim(edges, start, ROWS, 0)
        targets = lax.dynamic_slice_in_dim(teacher, start, ROWS, 0)
        return grad_fn(params, inputs, targets)
    grads = lax.map(one_replica, jnp.arange(N_ADA * N_AVG, dtype=jnp.int32))
    grads = [g.reshape((N_ADA, N_AVG) + g.shape[1:]) for g in grads]
    for level in range(LEVELS):
        bit = LEVELS - 1 - level
        partner = np.arange(N_ADA) ^ 1 << bit
        combined = []
        for mine in grads:
            theirs = mine[partner]
            axes = tuple(range(2, mine.ndim))
            dot = lax.optimization_barrier(jnp.sum(mine * theirs, axis=axes, keepdims=True))
            norm_a = lax.optimization_barrier(jnp.sum(mine * mine, axis=axes, keepdims=True))
            norm_b = lax.optimization_barrier(jnp.sum(theirs * theirs, axis=axes, keepdims=True))
            combined.append((1.0 - dot / (2.0 * (norm_a + norm_eps))) * mine + (1.0 - dot / (2.0 * (norm_b + norm_eps))) * theirs)
        grads = combined
    means = [lax.optimization_barrier(jnp.mean(g[0], axis=0)) for g in grads]
    return tuple((p - step_rate * m for p, m in zip(params, means)))
```

```python
import functools

import jax
import jax.numpy as jnp
from jax import lax
from jax.experimental import pallas as pl
from jax.experimental.pallas import tpu as pltpu
from jax.sharding import PartitionSpec as P

norm_eps = 1e-06
step_rate = 2.0
prec = lax.Precision.HIGH


def local_loss(params, inputs, targets):
    w_first, b_first, w_second, b_second, norm_gain, norm_shift = params
    zfirst = jnp.dot(inputs, w_first, precision=prec, preferred_element_type=jnp.float32) + b_first
    hidden = zfirst * jax.nn.sigmoid(zfirst)
    zsecond = (
        jnp.dot(hidden, w_second, precision=prec, preferred_element_type=jnp.float32) + b_second
    )
    center = zsecond - jnp.mean(zsecond, axis=1, keepdims=True)
    spread = jnp.mean(center * center, axis=1, keepdims=True)
    output = center * lax.rsqrt(spread + 1e-05) * norm_gain + norm_shift
    return 0.5 * jnp.sum((output - targets) ** 2) / inputs.shape[0]


class Sizes:
    def __init__(self, n_ada, n_avg, width):
        self.n_ada, self.n_avg, self.width = n_ada, n_avg, width
        self.core = 2 if n_ada % 2 == 0 else 1
        self.y = n_ada // self.core
        self.x = self.y if n_avg % self.y == 0 else 1
        self.z = n_avg // self.x
        self.cols = width // self.x
        self.levels = n_ada.bit_length() - 1
        self.stat_rows = -(-3 * (n_ada // 2) // 8) * 8

    def tensor_copies(self):
        gather = 2 * (self.z - 1) + self.x - 1 + 2 * (self.y - 1) + self.y * (self.x - 1)
        gather += 2 * self.y * (self.core - 1)
        scatter = 2 * (self.x - 1) + 2 * (self.z - 1)
        return (1 + self.levels) * (self.n_ada - 1) + scatter + gather

    def copies(self):
        return 2 * self.tensor_copies() + self.n_ada - 1 + self.n_avg - 1


def chunk_of(rows):
    return next(c for c in (32, 16, 8) if rows % c == 0)


def over_chunks(rows, body, init=0):
    size = chunk_of(rows)

    def step(i, carry):
        return body(pl.ds(pl.multiple_of(i * size, size), size), carry)

    return lax.fori_loop(0, rows // size, step, init)


def folded(block):
    return jnp.sum(block.reshape(block.shape[0] // 8, 8, block.shape[1]), axis=0)


def coefficients(dot, norm_a, norm_b):
    return (
        1.0 - dot / (2.0 * (norm_a + norm_eps)),
        1.0 - dot / (2.0 * (norm_b + norm_eps)),
    )


def comm_kernel(sz, *refs):
    g_first, g_second, g_vec, out_first, out_second, out_vec = refs[:6]
    scratch = refs[6:]
    per_first, per_second = scratch[:8], scratch[8:16]
    vec_ada, vec_avg, send, recv, local_sem = scratch[16:]

    me, v = lax.axis_index("ada"), lax.axis_index("avg")
    y, core = me // sz.core, me % sz.core
    z, x = v // sz.x, v % sz.x

    def ada_peer(a):
        return {"ada": a, "avg": v}

    def avg_peer(b):
        return {"ada": me, "avg": b}

    barrier = pltpu.get_barrier_semaphore()
    peers = [ada_peer(lax.rem(me + k, sz.n_ada)) for k in range(1, sz.n_ada)]
    peers += [avg_peer(lax.rem(v + k, sz.n_avg)) for k in range(1, sz.n_avg)]
    for peer in peers:
        pl.semaphore_signal(barrier, inc=1, device_id=peer, device_id_type=pl.DeviceIdType.MESH)
    pl.semaphore_wait(barrier, len(peers))

    started = []

    def start(src, dst, peer):
        i = len(started)
        copy = pltpu.make_async_remote_copy(
            src_ref=src, dst_ref=dst, send_sem=send.at[i], recv_sem=recv.at[i],
            device_id=peer, device_id_type=pl.DeviceIdType.MESH,
        )
        copy.start()
        started.append(copy)
        return copy

    def arrived(copies):
        for copy in copies:
            copy.wait_recv()

    vec_copies = []
    for k in range(1, sz.n_ada):
        peer = lax.rem(me + k, sz.n_ada)
        vec_copies.append(start(g_vec, vec_ada.at[me], ada_peer(peer)))
    slices = {}
    own_copies = {}
    for t, (grad, per) in enumerate(((g_second, per_second), (g_first, per_first))):
        got = per[0]
        part = grad.shape[0] // sz.n_ada
        own_copies[t] = pltpu.make_async_copy(
            grad.at[pl.ds(pl.multiple_of(me * part, 8), part)], got.at[me], local_sem.at[t]
        )
        own_copies[t].start()
        slices[t] = []
        order = [k for k in range(1, sz.n_ada) if k >= sz.core] + list(range(1, sz.core))
        for k in order:
            peer = jnp.bitwise_xor(me, k)
            rows = pl.ds(pl.multiple_of(peer * part, 8), part)
            slices[t].append(start(grad.at[rows], got.at[me], ada_peer(peer)))

    vec_ada[me] = g_vec[...]
    arrived(vec_copies)
    items = [vec_ada[a] for a in range(sz.n_ada)]
    while len(items) > 1:
        half = len(items) // 2
        merged = []
        for a, b in zip(items[:half], items[half:]):
            dot = jnp.sum(a * b, axis=1, keepdims=True)
            norm_a = jnp.sum(a * a, axis=1, keepdims=True)
            norm_b = jnp.sum(b * b, axis=1, keepdims=True)
            coef_a, coef_b = coefficients(dot, norm_a, norm_b)
            merged.append(coef_a * a + coef_b * b)
        items = merged
    vec_avg[v] = items[0]
    vec_out = []
    for k in range(1, sz.n_avg):
        peer = lax.rem(v + k, sz.n_avg)
        vec_out.append(start(vec_avg.at[v], vec_avg.at[v], avg_peer(peer)))

    def tensor(t, grad, out, per):
        got, stats, x_a, sum_a, z_a, z_b, sum_b, x_b = per
        part = grad.shape[0] // sz.n_ada
        strip = part // 2
        piece = strip // sz.z
        cols = sz.cols
        own_copies[t].wait()
        arrived(slices[t])

        def combine(level):
            half = sz.n_ada >> (level + 1)
            mine = stats.at[level, me]
            mine[...] = jnp.zeros((sz.stat_rows, sz.width), jnp.float32)
            for p in range(half):

                def add(rows, carry):
                    a, b = got[p, rows], got[p + half, rows]
                    return (
                        carry[0] + folded(a * b),
                        carry[1] + folded(a * a),
                        carry[2] + folded(b * b),
                    )

                zero = jnp.zeros((8, sz.width), jnp.float32)
                sums = over_chunks(part, add, (zero, zero, zero))
                for j, total in enumerate(sums):
                    row = 3 * p + j
                    mine[row : row + 1, :] = jnp.sum(total, axis=0, keepdims=True)
            copies = []
            for k in range(1, sz.n_ada):
                peer = lax.rem(me + k, sz.n_ada)
                copies.append(start(stats.at[level, me], stats.at[level, me], ada_peer(peer)))
            arrived(copies)
            total = stats[level, 0]
            for a in range(1, sz.n_ada):
                total = total + stats[level, a]
            total = jnp.sum(total, axis=1, keepdims=True)
            for p in range(half):
                coef_a, coef_b = coefficients(
                    total[3 * p : 3 * p + 1], total[3 * p + 1 : 3 * p + 2],
                    total[3 * p + 2 : 3 * p + 3],
                )

                def merge(rows, carry):
                    got[p, rows] = coef_a * got[p, rows] + coef_b * got[p + half, rows]
                    return carry

                over_chunks(part, merge)

        for level in range(sz.levels):
            combine(level)

        def at_x(i):
            return pl.ds(pl.multiple_of(i * cols, 128), cols)

        def at_z(i, base=0):
            return pl.ds(pl.multiple_of(base + i * piece, 8), piece)

        def z_peer(k):
            return lax.rem(z + k, sz.z)

        def x_peer(k):
            return lax.rem(x + k, sz.x)

        def z_dev(i):
            return avg_peer(i * sz.x + x)

        def x_dev(i):
            return avg_peer(z * sz.x + i)

        def total(rows, read, buffer, write):
            def body(window, carry):
                value = read(window)
                for k in range(buffer.shape[0]):
                    value = value + buffer[k, window]
                write(window, value)
                return carry

            over_chunks(rows, body)

        def shifted(window, base):
            return pl.ds(pl.multiple_of(base + window.start, 8), window.size)

        whole = got.at[0]
        a_x = [
            start(whole.at[pl.ds(0, strip), at_x(x_peer(k))], x_a.at[k - 1], x_dev(x_peer(k)))
            for k in range(1, sz.x)
        ]
        b_z = [
            start(whole.at[at_z(z_peer(k), strip)], z_b.at[k - 1], z_dev(z_peer(k)))
            for k in range(1, sz.z)
        ]

        def put(ref):
            def write(window, value):
                ref[window] = value

            return write

        def put_out(base):
            def write(window, value):
                out[shifted(window, base), at_x(x)] = value

            return write

        arrived(a_x)
        total(strip, lambda w: got[0, w, at_x(x)], x_a, put(sum_a))
        a_z = [
            start(sum_a.at[at_z(z_peer(k))], z_a.at[k - 1], z_dev(z_peer(k)))
            for k in range(1, sz.z)
        ]
        arrived(b_z)
        total(piece, lambda w: got[0, shifted(w, strip + z * piece)], z_b, put(sum_b))
        b_x = [
            start(sum_b.at[:, at_x(x_peer(k))], x_b.at[k - 1], x_dev(x_peer(k)))
            for k in range(1, sz.x)
        ]

        def base_of(side, row_y):
            return (row_y * sz.core + core) * part + side * strip

        def spread(side, row_y, columns, peer):
            rows = pl.ds(pl.multiple_of(base_of(side, row_y), 8), strip)
            block = out.at[rows] if columns is None else out.at[rows, columns]
            return start(block, block, peer)

        def spread_z(side):
            block = out.at[at_z(z, base_of(side, y)), at_x(x)]
            return [start(block, block, z_dev(z_peer(k))) for k in range(1, sz.z)]

        def y_row(k):
            return lax.rem(y + k, sz.y)

        def spread_y(side, columns):
            return [
                spread(side, y, columns, ada_peer(y_row(k) * sz.core + core))
                for k in range(1, sz.y)
            ]

        def spread_x(side, row_y):
            return [spread(side, row_y, at_x(x), x_dev(x_peer(k))) for k in range(1, sz.x)]

        def spread_core(side, row_y):
            return [
                spread(side, row_y, None, ada_peer(y * sz.core + lax.rem(core + k, sz.core)))
                for k in range(1, sz.core)
            ]

        arrived(a_z)
        total(piece, lambda w: sum_a[shifted(w, z * piece)], z_a, put_out(base_of(0, y) + z * piece))
        a_gather = spread_z(0)
        arrived(b_x)
        total(piece, lambda w: sum_b[w, at_x(x)], x_b, put_out(base_of(1, y) + z * piece))
        b_gather = spread_z(1)

        arrived(a_gather)
        a_x = spread_x(0, y)
        arrived(b_gather)
        b_y = spread_y(1, at_x(x))
        b_x = spread_x(1, y)
        arrived(a_x)
        a_y = spread_y(0, None)
        last = spread_core(0, y)
        arrived(b_y)
        b_x_far = []
        for k in range(1, sz.y):
            b_x_far += spread_x(1, y_row(k))
        arrived(b_x)
        last += spread_core(1, y)
        arrived(a_y)
        for k in range(1, sz.y):
            last += spread_core(0, y_row(k))
        arrived(b_x_far)
        for k in range(1, sz.y):
            last += spread_core(1, y_row(k))
        return last

    last = tensor(0, g_second, out_second, per_second)
    arrived(vec_out)
    vec_total = vec_avg[0]
    for b in range(1, sz.n_avg):
        vec_total = vec_total + vec_avg[b]
    out_vec[...] = vec_total
    last += tensor(1, g_first, out_first, per_first)
    arrived(last)
    for copy in started:
        copy.wait_send()


def tensor_scratch(sz, rows):
    part = rows // sz.n_ada
    strip = part // 2
    piece = strip // sz.z

    def vmem(*shape):
        return pltpu.VMEM(shape, jnp.float32)

    return [
        vmem(sz.n_ada, part, sz.width),
        vmem(sz.levels, sz.n_ada, sz.stat_rows, sz.width),
        vmem(max(sz.x - 1, 1), strip, sz.cols),
        vmem(strip, sz.cols),
        vmem(max(sz.z - 1, 1), piece, sz.cols),
        vmem(max(sz.z - 1, 1), piece, sz.width),
        vmem(piece, sz.width),
        vmem(max(sz.x - 1, 1), piece, sz.cols),
    ]


def adasum_totals(first, second, vectors):
    sz = Sizes(lax.axis_size("ada"), lax.axis_size("avg"), first.shape[1])
    in_vmem = pl.BlockSpec(memory_space=pltpu.VMEM)
    anywhere = pl.BlockSpec(memory_space=pl.ANY)
    return pl.pallas_call(
        functools.partial(comm_kernel, sz),
        out_shape=[jax.ShapeDtypeStruct(a.shape, a.dtype) for a in (first, second, vectors)],
        in_specs=[anywhere, anywhere, in_vmem],
        out_specs=[in_vmem] * 3,
        scratch_shapes=tensor_scratch(sz, first.shape[0])
        + tensor_scratch(sz, second.shape[0])
        + [
            pltpu.VMEM((sz.n_ada,) + vectors.shape, jnp.float32),
            pltpu.VMEM((sz.n_avg,) + vectors.shape, jnp.float32),
            pltpu.SemaphoreType.DMA((sz.copies(),)),
            pltpu.SemaphoreType.DMA((sz.copies(),)),
            pltpu.SemaphoreType.DMA((2,)),
        ],
        compiler_params=pltpu.CompilerParams(
            collective_id=0, has_side_effects=True, vmem_limit_bytes=40 * 2**20
        ),
        name="adasum_totals",
    )(first, second, vectors)


def local(edges, teacher, w_first, b_first, w_second, b_second, norm_gain, norm_shift):
    params = (w_first, b_first, w_second, b_second, norm_gain, norm_shift)
    grads = jax.grad(local_loss)(params, edges, teacher)
    vectors = jnp.stack([grads[1], grads[3], grads[4], grads[5]])
    vectors = jnp.concatenate([vectors, jnp.zeros_like(vectors)], axis=0)
    first, second, vec = adasum_totals(grads[0], grads[2], vectors)
    avg_count = lax.axis_size("avg")

    def new(param, total):
        return param - step_rate * (total / avg_count)

    return (
        new(w_first, first),
        new(b_first, vec[0]),
        new(w_second, second),
        new(b_second, vec[1]),
        new(norm_gain, vec[2]),
        new(norm_shift, vec[3]),
    )


def solution(mesh):
    in_specs = (P(("ada", "avg"), None), P(("ada", "avg"), None), P(), P(), P(), P(), P(), P())
    out_specs = (P(), P(), P(), P(), P(), P())
    return jax.shard_map(local, mesh=mesh, in_specs=in_specs, out_specs=out_specs, check_vma=False)
```

```python
import functools

import jax
import jax.numpy as jnp
from jax import lax
from jax.experimental import pallas as pl
from jax.experimental.pallas import tpu as pltpu
from jax.sharding import PartitionSpec as P

norm_eps = 1e-06
step_rate = 2.0
prec = lax.Precision.HIGH


def local_loss(params, inputs, targets):
    w_first, b_first, w_second, b_second, norm_gain, norm_shift = params
    zfirst = jnp.dot(inputs, w_first, precision=prec, preferred_element_type=jnp.float32) + b_first
    hidden = zfirst * jax.nn.sigmoid(zfirst)
    zsecond = (
        jnp.dot(hidden, w_second, precision=prec, preferred_element_type=jnp.float32) + b_second
    )
    center = zsecond - jnp.mean(zsecond, axis=1, keepdims=True)
    spread = jnp.mean(center * center, axis=1, keepdims=True)
    output = center * lax.rsqrt(spread + 1e-05) * norm_gain + norm_shift
    return 0.5 * jnp.sum((output - targets) ** 2) / inputs.shape[0]


class Sizes:
    def __init__(self, n_ada, n_avg, width):
        self.n_ada, self.n_avg, self.width = n_ada, n_avg, width
        self.core = 2 if n_ada % 2 == 0 else 1
        self.y = n_ada // self.core
        self.x = self.y if n_avg % self.y == 0 else 1
        self.z = n_avg // self.x
        self.cols = width // self.x
        self.stat_rows = -(-(n_ada * (n_ada + 1) // 2) // 8) * 8

    def tensor_copies(self):
        gather = 2 * (self.z - 1) + self.x - 1 + 2 * (self.y - 1) + self.y * (self.x - 1)
        gather += 2 * self.y * (self.core - 1)
        scatter = 2 * (self.x - 1) + 2 * (self.z - 1)
        return 2 * (self.n_ada - 1) + scatter + gather

    def copies(self):
        return 2 * self.tensor_copies() + self.n_ada - 1 + self.n_avg - 1


def chunk_of(rows):
    return next(c for c in (32, 16, 8) if rows % c == 0)


def over_chunks(rows, body, init=0, size=None):
    size = size or chunk_of(rows)

    def step(i, carry):
        return body(pl.ds(pl.multiple_of(i * size, size), size), carry)

    return lax.fori_loop(0, rows // size, step, init)


def folded(block):
    return jnp.sum(block.reshape(block.shape[0] // 8, 8, block.shape[1]), axis=0)


def coefficients(dot, norm_a, norm_b):
    return (
        1.0 - dot / (2.0 * (norm_a + norm_eps)),
        1.0 - dot / (2.0 * (norm_b + norm_eps)),
    )


def adasum_weights(inner, count):
    def product(i, j):
        return inner[min(i, j), max(i, j)]

    weights = [{a: jnp.ones((1, 1), jnp.float32)} for a in range(count)]
    while count > 1:
        half = count // 2
        coefs = [
            coefficients(product(p, p + half), product(p, p), product(p + half, p + half))
            for p in range(half)
        ]
        merged, following = [], {}
        for p in range(half):
            both = {a: coefs[p][0] * w for a, w in weights[p].items()}
            both.update({a: coefs[p][1] * w for a, w in weights[p + half].items()})
            merged.append(both)
            for q in range(p, half):
                value = 0.0
                for i, left in zip((p, p + half), coefs[p]):
                    for j, right in zip((q, q + half), coefs[q]):
                        value = value + left * right * product(i, j)
                following[p, q] = jnp.maximum(value, 0.0) if p == q else value
        weights, inner, count = merged, following, half
    return [weights[0][a] for a in sorted(weights[0])]


def comm_kernel(sz, *refs):
    g_first, g_second, g_vec, out_first, out_second, out_vec = refs[:6]
    scratch = refs[6:]
    per_first, per_second = scratch[:8], scratch[8:16]
    vec_ada, vec_avg, send, recv, local_sem = scratch[16:]

    me, v = lax.axis_index("ada"), lax.axis_index("avg")
    y, core = me // sz.core, me % sz.core
    z, x = v // sz.x, v % sz.x

    def ada_peer(a):
        return {"ada": a, "avg": v}

    def avg_peer(b):
        return {"ada": me, "avg": b}

    barrier = pltpu.get_barrier_semaphore()
    peers = [ada_peer(lax.rem(me + k, sz.n_ada)) for k in range(1, sz.n_ada)]
    peers += [avg_peer(lax.rem(v + k, sz.n_avg)) for k in range(1, sz.n_avg)]
    for peer in peers:
        pl.semaphore_signal(barrier, inc=1, device_id=peer, device_id_type=pl.DeviceIdType.MESH)
    pl.semaphore_wait(barrier, len(peers))

    started = []

    def start(src, dst, peer):
        i = len(started)
        copy = pltpu.make_async_remote_copy(
            src_ref=src, dst_ref=dst, send_sem=send.at[i], recv_sem=recv.at[i],
            device_id=peer, device_id_type=pl.DeviceIdType.MESH,
        )
        copy.start()
        started.append(copy)
        return copy

    def arrived(copies):
        for copy in copies:
            copy.wait_recv()

    vec_copies = []
    for k in range(1, sz.n_ada):
        peer = lax.rem(me + k, sz.n_ada)
        vec_copies.append(start(g_vec, vec_ada.at[me], ada_peer(peer)))
    sides = ((g_second, per_second), (g_first, per_first))
    own_copies = []
    slices = ([], [])
    for t, (grad, per) in enumerate(sides):
        part = grad.shape[0] // sz.n_ada
        rows = pl.ds(pl.multiple_of(me * part, 8), part)
        own_copies.append(
            pltpu.make_async_copy(grad.at[rows], per[0].at[me], local_sem.at[t])
        )
        own_copies[t].start()

    def give(t, offsets):
        grad, per = sides[t]
        part = grad.shape[0] // sz.n_ada
        for k in offsets:
            peer = jnp.bitwise_xor(me, k)
            rows = pl.ds(pl.multiple_of(peer * part, 8), part)
            slices[t].append(start(grad.at[rows], per[0].at[me], ada_peer(peer)))

    far, near = list(range(sz.core, sz.n_ada)), list(range(1, sz.core))
    cut = len(far) // 2
    give(0, far + near)
    give(1, far[:cut] + near)

    vec_ada[me] = g_vec[...]
    arrived(vec_copies)
    items = [vec_ada[a] for a in range(sz.n_ada)]
    while len(items) > 1:
        half = len(items) // 2
        merged = []
        for a, b in zip(items[:half], items[half:]):
            dot = jnp.sum(a * b, axis=1, keepdims=True)
            norm_a = jnp.sum(a * a, axis=1, keepdims=True)
            norm_b = jnp.sum(b * b, axis=1, keepdims=True)
            coef_a, coef_b = coefficients(dot, norm_a, norm_b)
            merged.append(coef_a * a + coef_b * b)
        items = merged
    vec_avg[v] = items[0]
    vec_out = []
    for k in range(1, sz.n_avg):
        peer = lax.rem(v + k, sz.n_avg)
        vec_out.append(start(vec_avg.at[v], vec_avg.at[v], avg_peer(peer)))

    def tensor(t, grad, out, per):
        got, stats, x_a, sum_a, z_a, z_b, sum_b, x_b = per
        part = grad.shape[0] // sz.n_ada
        strip = part // 2
        piece = strip // sz.z
        cols = sz.cols
        own_copies[t].wait()
        arrived(slices[t])

        pairs = [(i, j) for i in range(sz.n_ada) for j in range(i, sz.n_ada)]
        mine = stats.at[me]
        mine[...] = jnp.zeros((sz.stat_rows, sz.width), jnp.float32)
        for some in (pairs[i : i + 5] for i in range(0, len(pairs), 5)):

            def add(rows, carry):
                used = {i: got[i, rows] for pair in some for i in pair}
                return tuple(c + folded(used[i] * used[j]) for c, (i, j) in zip(carry, some))

            zero = jnp.zeros((8, sz.width), jnp.float32)
            sums = over_chunks(part, add, (zero,) * len(some), 8)
            for pair, value in zip(some, sums):
                row = pairs.index(pair)
                mine[row : row + 1, :] = jnp.sum(value, axis=0, keepdims=True)
        stat_copies = []
        for k in range(1, sz.n_ada):
            peer = lax.rem(me + k, sz.n_ada)
            stat_copies.append(start(stats.at[me], stats.at[me], ada_peer(peer)))
        yield
        arrived(stat_copies)
        gathered = stats[0]
        for a in range(1, sz.n_ada):
            gathered = gathered + stats[a]
        gathered = jnp.sum(gathered, axis=1, keepdims=True)
        weights = adasum_weights(
            {pair: gathered[row : row + 1] for row, pair in enumerate(pairs)}, sz.n_ada
        )

        def merge(rows, carry):
            value = weights[0] * got[0, rows]
            for a in range(1, sz.n_ada):
                value = value + weights[a] * got[a, rows]
            got[0, rows] = value
            return carry

        over_chunks(part, merge)

        def at_x(i):
            return pl.ds(pl.multiple_of(i * cols, 128), cols)

        def at_z(i, base=0):
            return pl.ds(pl.multiple_of(base + i * piece, 8), piece)

        def z_peer(k):
            return lax.rem(z + k, sz.z)

        def x_peer(k):
            return lax.rem(x + k, sz.x)

        def z_dev(i):
            return avg_peer(i * sz.x + x)

        def x_dev(i):
            return avg_peer(z * sz.x + i)

        def total(rows, read, buffer, write):
            def body(window, carry):
                value = read(window)
                for k in range(buffer.shape[0]):
                    value = value + buffer[k, window]
                write(window, value)
                return carry

            over_chunks(rows, body)

        def shifted(window, base):
            return pl.ds(pl.multiple_of(base + window.start, 8), window.size)

        whole = got.at[0]
        a_x = [
            start(whole.at[pl.ds(0, strip), at_x(x_peer(k))], x_a.at[k - 1], x_dev(x_peer(k)))
            for k in range(1, sz.x)
        ]
        b_z = [
            start(whole.at[at_z(z_peer(k), strip)], z_b.at[k - 1], z_dev(z_peer(k)))
            for k in range(1, sz.z)
        ]

        def put(ref):
            def write(window, value):
                ref[window] = value

            return write

        def put_out(base):
            def write(window, value):
                out[shifted(window, base), at_x(x)] = value

            return write

        yield
        arrived(a_x)
        total(strip, lambda w: got[0, w, at_x(x)], x_a, put(sum_a))
        a_z = [
            start(sum_a.at[at_z(z_peer(k))], z_a.at[k - 1], z_dev(z_peer(k)))
            for k in range(1, sz.z)
        ]
        yield
        arrived(b_z)
        total(piece, lambda w: got[0, shifted(w, strip + z * piece)], z_b, put(sum_b))
        b_x = [
            start(sum_b.at[:, at_x(x_peer(k))], x_b.at[k - 1], x_dev(x_peer(k)))
            for k in range(1, sz.x)
        ]

        def base_of(side, row_y):
            return (row_y * sz.core + core) * part + side * strip

        def spread(side, row_y, columns, peer):
            rows = pl.ds(pl.multiple_of(base_of(side, row_y), 8), strip)
            block = out.at[rows] if columns is None else out.at[rows, columns]
            return start(block, block, peer)

        def spread_z(side):
            block = out.at[at_z(z, base_of(side, y)), at_x(x)]
            return [start(block, block, z_dev(z_peer(k))) for k in range(1, sz.z)]

        def y_row(k):
            return lax.rem(y + k, sz.y)

        def spread_y(side, columns):
            return [
                spread(side, y, columns, ada_peer(y_row(k) * sz.core + core))
                for k in range(1, sz.y)
            ]

        def spread_x(side, row_y):
            return [spread(side, row_y, at_x(x), x_dev(x_peer(k))) for k in range(1, sz.x)]

        def spread_core(side, row_y):
            return [
                spread(side, row_y, None, ada_peer(y * sz.core + lax.rem(core + k, sz.core)))
                for k in range(1, sz.core)
            ]

        yield
        arrived(a_z)
        total(piece, lambda w: sum_a[shifted(w, z * piece)], z_a, put_out(base_of(0, y) + z * piece))
        a_gather = spread_z(0)
        yield
        arrived(b_x)
        total(piece, lambda w: sum_b[w, at_x(x)], x_b, put_out(base_of(1, y) + z * piece))
        b_gather = spread_z(1)

        yield
        arrived(a_gather)
        a_x = spread_x(0, y)
        yield
        arrived(b_gather)
        b_y = spread_y(1, at_x(x))
        b_x = spread_x(1, y)
        yield
        arrived(a_x)
        a_y = spread_y(0, None)
        last = spread_core(0, y)
        yield
        arrived(b_y)
        b_x_far = []
        for k in range(1, sz.y):
            b_x_far += spread_x(1, y_row(k))
        yield
        arrived(b_x)
        last += spread_core(1, y)
        yield
        arrived(a_y)
        for k in range(1, sz.y):
            last += spread_core(0, y_row(k))
        yield
        arrived(b_x_far)
        for k in range(1, sz.y):
            last += spread_core(1, y_row(k))
        yield
        arrived(last)

    second = tensor(0, g_second, out_second, per_second)
    first = tensor(1, g_first, out_first, per_first)
    next(second)
    give(1, far[cut:])
    for _ in range(5):
        next(second)
    arrived(vec_out)
    vec_total = vec_avg[0]
    for b in range(1, sz.n_avg):
        vec_total = vec_total + vec_avg[b]
    out_vec[...] = vec_total
    running = [first, second]
    while running:
        running = [one for one in running if next(one, True) is None]

    for copy in started:
        copy.wait_send()


def tensor_scratch(sz, rows):
    part = rows // sz.n_ada
    strip = part // 2
    piece = strip // sz.z

    def vmem(*shape):
        return pltpu.VMEM(shape, jnp.float32)

    return [
        vmem(sz.n_ada, part, sz.width),
        vmem(sz.n_ada, sz.stat_rows, sz.width),
        vmem(max(sz.x - 1, 1), strip, sz.cols),
        vmem(strip, sz.cols),
        vmem(max(sz.z - 1, 1), piece, sz.cols),
        vmem(max(sz.z - 1, 1), piece, sz.width),
        vmem(piece, sz.width),
        vmem(max(sz.x - 1, 1), piece, sz.cols),
    ]


def adasum_totals(first, second, vectors):
    sz = Sizes(lax.axis_size("ada"), lax.axis_size("avg"), first.shape[1])
    in_vmem = pl.BlockSpec(memory_space=pltpu.VMEM)
    anywhere = pl.BlockSpec(memory_space=pl.ANY)
    return pl.pallas_call(
        functools.partial(comm_kernel, sz),
        out_shape=[jax.ShapeDtypeStruct(a.shape, a.dtype) for a in (first, second, vectors)],
        in_specs=[anywhere, anywhere, in_vmem],
        out_specs=[in_vmem] * 3,
        scratch_shapes=tensor_scratch(sz, first.shape[0])
        + tensor_scratch(sz, second.shape[0])
        + [
            pltpu.VMEM((sz.n_ada,) + vectors.shape, jnp.float32),
            pltpu.VMEM((sz.n_avg,) + vectors.shape, jnp.float32),
            pltpu.SemaphoreType.DMA((sz.copies(),)),
            pltpu.SemaphoreType.DMA((sz.copies(),)),
            pltpu.SemaphoreType.DMA((2,)),
        ],
        compiler_params=pltpu.CompilerParams(
            collective_id=0, has_side_effects=True, vmem_limit_bytes=40 * 2**20
        ),
        name="adasum_totals",
    )(first, second, vectors)


def local(edges, teacher, w_first, b_first, w_second, b_second, norm_gain, norm_shift):
    params = (w_first, b_first, w_second, b_second, norm_gain, norm_shift)
    grads = jax.grad(local_loss)(params, edges, teacher)
    vectors = jnp.stack([grads[1], grads[3], grads[4], grads[5]])
    vectors = jnp.concatenate([vectors, jnp.zeros_like(vectors)], axis=0)
    first, second, vec = adasum_totals(grads[0], grads[2], vectors)
    avg_count = lax.axis_size("avg")

    def new(param, total):
        return param - step_rate * (total / avg_count)

    return (
        new(w_first, first),
        new(b_first, vec[0]),
        new(w_second, second),
        new(b_second, vec[1]),
        new(norm_gain, vec[2]),
        new(norm_shift, vec[3]),
    )


def solution(mesh):
    in_specs = (P(("ada", "avg"), None), P(("ada", "avg"), None), P(), P(), P(), P(), P(), P())
    out_specs = (P(), P(), P(), P(), P(), P())
    return jax.shard_map(local, mesh=mesh, in_specs=in_specs, out_specs=out_specs, check_vma=False)
```

```python
import functools

import jax
import jax.numpy as jnp
from jax import lax
from jax.experimental import pallas as pl
from jax.experimental.pallas import tpu as pltpu
from jax.sharding import PartitionSpec as P

norm_eps = 1e-06
step_rate = 2.0
prec = lax.Precision.HIGH


def local_loss(params, first_sums, targets):
    w_second, b_second, norm_gain, norm_shift = params
    hidden = first_sums * jax.nn.sigmoid(first_sums)
    zsecond = (
        jnp.dot(hidden, w_second, precision=prec, preferred_element_type=jnp.float32) + b_second
    )
    center = zsecond - jnp.mean(zsecond, axis=1, keepdims=True)
    spread = jnp.mean(center * center, axis=1, keepdims=True)
    output = center * lax.rsqrt(spread + 1e-05) * norm_gain + norm_shift
    return 0.5 * jnp.sum((output - targets) ** 2) / first_sums.shape[0]


class Sizes:
    def __init__(self, n_ada, n_avg, width):
        self.n_ada, self.n_avg, self.width = n_ada, n_avg, width
        self.core = 2 if n_ada % 2 == 0 else 1
        self.y = n_ada // self.core
        self.x = self.y if n_avg % self.y == 0 else 1
        self.z = n_avg // self.x
        self.cols = width // self.x
        self.stat_rows = -(-(n_ada * (n_ada + 1) // 2) // 8) * 8

    def tensor_copies(self):
        gather = 2 * (self.z - 1) + self.x - 1 + 2 * (self.y - 1) + self.y * (self.x - 1)
        gather += 2 * self.y * (self.core - 1)
        scatter = 2 * (self.x - 1) + 2 * (self.z - 1)
        return 2 * (self.n_ada - 1) + scatter + gather

    def copies(self):
        return 2 * self.tensor_copies() + self.n_ada - 1 + self.n_avg - 1


def chunk_of(rows):
    return next(c for c in (32, 16, 8) if rows % c == 0)


def over_chunks(rows, body, init=0, size=None):
    size = size or chunk_of(rows)

    def step(i, carry):
        return body(pl.ds(pl.multiple_of(i * size, size), size), carry)

    return lax.fori_loop(0, rows // size, step, init)


def folded(block):
    return jnp.sum(block.reshape(block.shape[0] // 8, 8, block.shape[1]), axis=0)


def split(value):
    high = value.astype(jnp.bfloat16)
    return high, (value - high.astype(jnp.float32)).astype(jnp.bfloat16)


def contracted(left, right):
    return lax.dot_general(
        left, right, (((0,), (0,)), ((), ())), preferred_element_type=jnp.float32
    )


def coefficients(dot, norm_a, norm_b):
    return (
        1.0 - dot / (2.0 * (norm_a + norm_eps)),
        1.0 - dot / (2.0 * (norm_b + norm_eps)),
    )


def adasum_weights(inner, count):
    def product(i, j):
        return inner[min(i, j), max(i, j)]

    weights = [{a: jnp.ones((1, 1), jnp.float32)} for a in range(count)]
    while count > 1:
        half = count // 2
        coefs = [
            coefficients(product(p, p + half), product(p, p), product(p + half, p + half))
            for p in range(half)
        ]
        merged, following = [], {}
        for p in range(half):
            both = {a: coefs[p][0] * w for a, w in weights[p].items()}
            both.update({a: coefs[p][1] * w for a, w in weights[p + half].items()})
            merged.append(both)
            for q in range(p, half):
                value = 0.0
                for i, left in zip((p, p + half), coefs[p]):
                    for j, right in zip((q, q + half), coefs[q]):
                        value = value + left * right * product(i, j)
                following[p, q] = jnp.maximum(value, 0.0) if p == q else value
        weights, inner, count = merged, following, half
    return [weights[0][a] for a in sorted(weights[0])]


def comm_kernel(sz, *refs):
    x_ref, dz_ref, g_second, g_vec, out_first, out_second, out_vec = refs[:7]
    scratch = refs[7:]
    per_first, per_second = scratch[:8], scratch[8:16]
    vec_ada, vec_avg, send, recv, local_sem = scratch[16:21]
    g_first, x_buf, dz_high, dz_low, x_sem = scratch[21:]

    me, v = lax.axis_index("ada"), lax.axis_index("avg")
    y, core = me // sz.core, me % sz.core
    z, x = v // sz.x, v % sz.x

    def ada_peer(a):
        return {"ada": a, "avg": v}

    def avg_peer(b):
        return {"ada": me, "avg": b}

    sub = x_buf.shape[2]
    chunk = x_ref.shape[1] // sz.y
    firsts = [
        jnp.bitwise_xor(y, k) * chunk + i * sub
        for k in list(range(1, sz.y)) + [0]
        for i in range(chunk // sub)
    ]
    loads = [
        pltpu.make_async_copy(
            x_ref.at[:, pl.ds(pl.multiple_of(first, 128), sub)],
            x_buf.at[i % 2], x_sem.at[i % 2],
        )
        for i, first in enumerate(firsts)
    ]
    for load in loads[:2]:
        load.start()

    def weight_grad(i):
        loads[i].wait()
        high, low = split(x_buf[i % 2])
        if i + 2 < len(loads):
            loads[i + 2].start()
        value = contracted(high, dz_low[...]) + contracted(low, dz_high[...])
        rows = pl.ds(pl.multiple_of(firsts[i], 8), sub)
        g_first[rows] = value + contracted(high, dz_high[...])

    barrier = pltpu.get_barrier_semaphore()
    peers = [ada_peer(lax.rem(me + k, sz.n_ada)) for k in range(1, sz.n_ada)]
    peers += [avg_peer(lax.rem(v + k, sz.n_avg)) for k in range(1, sz.n_avg)]
    for peer in peers:
        pl.semaphore_signal(barrier, inc=1, device_id=peer, device_id_type=pl.DeviceIdType.MESH)
    pl.semaphore_wait(barrier, len(peers))

    started = []

    def start(src, dst, peer):
        i = len(started)
        copy = pltpu.make_async_remote_copy(
            src_ref=src, dst_ref=dst, send_sem=send.at[i], recv_sem=recv.at[i],
            device_id=peer, device_id_type=pl.DeviceIdType.MESH,
        )
        copy.start()
        started.append(copy)
        return copy

    def arrived(copies):
        for copy in copies:
            copy.wait_recv()

    vec_copies = []
    for k in range(1, sz.n_ada):
        peer = lax.rem(me + k, sz.n_ada)
        vec_copies.append(start(g_vec, vec_ada.at[me], ada_peer(peer)))
    sides = ((g_second, per_second), (g_first, per_first))
    own_copies = []
    slices = ([], [])
    for t, (grad, per) in enumerate(sides):
        part = grad.shape[0] // sz.n_ada
        rows = pl.ds(pl.multiple_of(me * part, 8), part)
        own_copies.append(
            pltpu.make_async_copy(grad.at[rows], per[0].at[me], local_sem.at[t])
        )
    own_copies[0].start()

    def give(t, offsets):
        grad, per = sides[t]
        part = grad.shape[0] // sz.n_ada
        for k in offsets:
            peer = jnp.bitwise_xor(me, k)
            rows = pl.ds(pl.multiple_of(peer * part, 8), part)
            slices[t].append(start(grad.at[rows], per[0].at[me], ada_peer(peer)))

    far, near = list(range(sz.core, sz.n_ada)), list(range(1, sz.core))
    cut = len(far) // 2
    give(0, far + near)

    def split_rows(rows, carry):
        dz_high[rows], dz_low[rows] = split(dz_ref[rows])
        return carry

    over_chunks(dz_ref.shape[0], split_rows)
    away = len(loads) - chunk // sub
    for i in range(away):
        weight_grad(i)
    give(1, far[:cut])
    for i in range(away, len(loads)):
        weight_grad(i)
    give(1, near)
    own_copies[1].start()

    vec_ada[me] = g_vec[...]
    arrived(vec_copies)
    items = [vec_ada[a] for a in range(sz.n_ada)]
    while len(items) > 1:
        half = len(items) // 2
        merged = []
        for a, b in zip(items[:half], items[half:]):
            dot = jnp.sum(a * b, axis=1, keepdims=True)
            norm_a = jnp.sum(a * a, axis=1, keepdims=True)
            norm_b = jnp.sum(b * b, axis=1, keepdims=True)
            coef_a, coef_b = coefficients(dot, norm_a, norm_b)
            merged.append(coef_a * a + coef_b * b)
        items = merged
    vec_avg[v] = items[0]
    vec_out = []
    for k in range(1, sz.n_avg):
        peer = lax.rem(v + k, sz.n_avg)
        vec_out.append(start(vec_avg.at[v], vec_avg.at[v], avg_peer(peer)))

    def tensor(t, grad, out, per):
        got, stats, x_a, sum_a, z_a, z_b, sum_b, x_b = per
        part = grad.shape[0] // sz.n_ada
        strip = part // 2
        piece = strip // sz.z
        cols = sz.cols
        own_copies[t].wait()
        arrived(slices[t])

        pairs = [(i, j) for i in range(sz.n_ada) for j in range(i, sz.n_ada)]
        mine = stats.at[me]
        mine[...] = jnp.zeros((sz.stat_rows, sz.width), jnp.float32)
        for some in (pairs[i : i + 5] for i in range(0, len(pairs), 5)):

            def add(rows, carry):
                used = {i: got[i, rows] for pair in some for i in pair}
                return tuple(c + folded(used[i] * used[j]) for c, (i, j) in zip(carry, some))

            zero = jnp.zeros((8, sz.width), jnp.float32)
            sums = over_chunks(part, add, (zero,) * len(some), 8)
            for pair, value in zip(some, sums):
                row = pairs.index(pair)
                mine[row : row + 1, :] = jnp.sum(value, axis=0, keepdims=True)
        stat_copies = []
        for k in range(1, sz.n_ada):
            peer = lax.rem(me + k, sz.n_ada)
            stat_copies.append(start(stats.at[me], stats.at[me], ada_peer(peer)))
        yield
        arrived(stat_copies)
        gathered = stats[0]
        for a in range(1, sz.n_ada):
            gathered = gathered + stats[a]
        gathered = jnp.sum(gathered, axis=1, keepdims=True)
        weights = adasum_weights(
            {pair: gathered[row : row + 1] for row, pair in enumerate(pairs)}, sz.n_ada
        )

        def merge(rows, carry):
            value = weights[0] * got[0, rows]
            for a in range(1, sz.n_ada):
                value = value + weights[a] * got[a, rows]
            got[0, rows] = value
            return carry

        over_chunks(part, merge)

        def at_x(i):
            return pl.ds(pl.multiple_of(i * cols, 128), cols)

        def at_z(i, base=0):
            return pl.ds(pl.multiple_of(base + i * piece, 8), piece)

        def z_peer(k):
            return lax.rem(z + k, sz.z)

        def x_peer(k):
            return lax.rem(x + k, sz.x)

        def z_dev(i):
            return avg_peer(i * sz.x + x)

        def x_dev(i):
            return avg_peer(z * sz.x + i)

        def total(rows, read, buffer, write):
            def body(window, carry):
                value = read(window)
                for k in range(buffer.shape[0]):
                    value = value + buffer[k, window]
                write(window, value)
                return carry

            over_chunks(rows, body)

        def shifted(window, base):
            return pl.ds(pl.multiple_of(base + window.start, 8), window.size)

        whole = got.at[0]
        a_x = [
            start(whole.at[pl.ds(0, strip), at_x(x_peer(k))], x_a.at[k - 1], x_dev(x_peer(k)))
            for k in range(1, sz.x)
        ]
        b_z = [
            start(whole.at[at_z(z_peer(k), strip)], z_b.at[k - 1], z_dev(z_peer(k)))
            for k in range(1, sz.z)
        ]

        def put(ref):
            def write(window, value):
                ref[window] = value

            return write

        def put_out(base):
            def write(window, value):
                out[shifted(window, base), at_x(x)] = value

            return write

        yield
        arrived(a_x)
        total(strip, lambda w: got[0, w, at_x(x)], x_a, put(sum_a))
        a_z = [
            start(sum_a.at[at_z(z_peer(k))], z_a.at[k - 1], z_dev(z_peer(k)))
            for k in range(1, sz.z)
        ]
        yield
        arrived(b_z)
        total(piece, lambda w: got[0, shifted(w, strip + z * piece)], z_b, put(sum_b))
        b_x = [
            start(sum_b.at[:, at_x(x_peer(k))], x_b.at[k - 1], x_dev(x_peer(k)))
            for k in range(1, sz.x)
        ]

        def base_of(side, row_y):
            return (row_y * sz.core + core) * part + side * strip

        def spread(side, row_y, columns, peer):
            rows = pl.ds(pl.multiple_of(base_of(side, row_y), 8), strip)
            block = out.at[rows] if columns is None else out.at[rows, columns]
            return start(block, block, peer)

        def spread_z(side):
            block = out.at[at_z(z, base_of(side, y)), at_x(x)]
            return [start(block, block, z_dev(z_peer(k))) for k in range(1, sz.z)]

        def y_row(k):
            return lax.rem(y + k, sz.y)

        def spread_y(side, columns):
            return [
                spread(side, y, columns, ada_peer(y_row(k) * sz.core + core))
                for k in range(1, sz.y)
            ]

        def spread_x(side, row_y):
            return [spread(side, row_y, at_x(x), x_dev(x_peer(k))) for k in range(1, sz.x)]

        def spread_core(side, row_y):
            return [
                spread(side, row_y, None, ada_peer(y * sz.core + lax.rem(core + k, sz.core)))
                for k in range(1, sz.core)
            ]

        yield
        arrived(a_z)
        total(piece, lambda w: sum_a[shifted(w, z * piece)], z_a, put_out(base_of(0, y) + z * piece))
        a_gather = spread_z(0)
        yield
        arrived(b_x)
        total(piece, lambda w: sum_b[w, at_x(x)], x_b, put_out(base_of(1, y) + z * piece))
        b_gather = spread_z(1)

        yield
        arrived(a_gather)
        a_x = spread_x(0, y)
        yield
        arrived(b_gather)
        b_y = spread_y(1, at_x(x))
        b_x = spread_x(1, y)
        yield
        arrived(a_x)
        a_y = spread_y(0, None)
        last = spread_core(0, y)
        yield
        arrived(b_y)
        b_x_far = []
        for k in range(1, sz.y):
            b_x_far += spread_x(1, y_row(k))
        yield
        arrived(b_x)
        last += spread_core(1, y)
        yield
        arrived(a_y)
        for k in range(1, sz.y):
            last += spread_core(0, y_row(k))
        yield
        arrived(b_x_far)
        for k in range(1, sz.y):
            last += spread_core(1, y_row(k))
        yield
        arrived(last)

    second = tensor(0, g_second, out_second, per_second)
    first = tensor(1, g_first, out_first, per_first)
    next(second)
    give(1, far[cut:])
    for _ in range(5):
        next(second)
    arrived(vec_out)
    vec_total = vec_avg[0]
    for b in range(1, sz.n_avg):
        vec_total = vec_total + vec_avg[b]
    out_vec[...] = vec_total
    running = [first, second]
    while running:
        running = [one for one in running if next(one, True) is None]

    for copy in started:
        copy.wait_send()


def tensor_scratch(sz, rows):
    part = rows // sz.n_ada
    strip = part // 2
    piece = strip // sz.z

    def vmem(*shape):
        return pltpu.VMEM(shape, jnp.float32)

    return [
        vmem(sz.n_ada, part, sz.width),
        vmem(sz.n_ada, sz.stat_rows, sz.width),
        vmem(max(sz.x - 1, 1), strip, sz.cols),
        vmem(strip, sz.cols),
        vmem(max(sz.z - 1, 1), piece, sz.cols),
        vmem(max(sz.z - 1, 1), piece, sz.width),
        vmem(piece, sz.width),
        vmem(max(sz.x - 1, 1), piece, sz.cols),
    ]


def adasum_totals(edges, delta, second, vectors):
    sz = Sizes(lax.axis_size("ada"), lax.axis_size("avg"), delta.shape[1])
    rows, d_in = edges.shape
    chunk = d_in // sz.y
    sub = next(c for c in (384, 256, 128) if chunk % c == 0)
    first = jax.ShapeDtypeStruct((d_in, delta.shape[1]), jnp.float32)
    in_vmem = pl.BlockSpec(memory_space=pltpu.VMEM)
    anywhere = pl.BlockSpec(memory_space=pl.ANY)
    return pl.pallas_call(
        functools.partial(comm_kernel, sz),
        out_shape=[jax.ShapeDtypeStruct(a.shape, a.dtype) for a in (first, second, vectors)],
        in_specs=[anywhere, in_vmem, anywhere, in_vmem],
        out_specs=[in_vmem] * 3,
        scratch_shapes=tensor_scratch(sz, first.shape[0])
        + tensor_scratch(sz, second.shape[0])
        + [
            pltpu.VMEM((sz.n_ada,) + vectors.shape, jnp.float32),
            pltpu.VMEM((sz.n_avg,) + vectors.shape, jnp.float32),
            pltpu.SemaphoreType.DMA((sz.copies(),)),
            pltpu.SemaphoreType.DMA((sz.copies(),)),
            pltpu.SemaphoreType.DMA((2,)),
            pltpu.VMEM(first.shape, jnp.float32),
            pltpu.VMEM((2, rows, sub), jnp.float32),
            pltpu.VMEM(delta.shape, jnp.bfloat16),
            pltpu.VMEM(delta.shape, jnp.bfloat16),
            pltpu.SemaphoreType.DMA((2,)),
        ],
        compiler_params=pltpu.CompilerParams(
            collective_id=0, has_side_effects=True, vmem_limit_bytes=56 * 2**20
        ),
        name="adasum_totals",
    )(edges, delta, second, vectors)


def local(edges, teacher, w_first, b_first, w_second, b_second, norm_gain, norm_shift):
    first_sums = (
        jnp.dot(edges, w_first, precision=prec, preferred_element_type=jnp.float32) + b_first
    )
    params = (w_second, b_second, norm_gain, norm_shift)
    grads, delta = jax.grad(local_loss, argnums=(0, 1))(params, first_sums, teacher)
    vectors = jnp.stack([jnp.sum(delta, axis=0), grads[1], grads[2], grads[3]])
    vectors = jnp.concatenate([vectors, jnp.zeros_like(vectors)], axis=0)
    first, second, vec = adasum_totals(edges, delta, grads[0], vectors)
    avg_count = lax.axis_size("avg")

    def new(param, total):
        return param - step_rate * (total / avg_count)

    return (
        new(w_first, first),
        new(b_first, vec[0]),
        new(w_second, second),
        new(b_second, vec[1]),
        new(norm_gain, vec[2]),
        new(norm_shift, vec[3]),
    )


def solution(mesh):
    in_specs = (P(("ada", "avg"), None), P(("ada", "avg"), None), P(), P(), P(), P(), P(), P())
    out_specs = (P(), P(), P(), P(), P(), P())
    return jax.shard_map(local, mesh=mesh, in_specs=in_specs, out_specs=out_specs, check_vma=False)
```

```python
import functools

import jax
import jax.numpy as jnp
from jax import lax
from jax.experimental import pallas as pl
from jax.experimental.pallas import tpu as pltpu
from jax.sharding import PartitionSpec as P

norm_eps = 1e-06
step_rate = 2.0
prec = lax.Precision.HIGH


def local_loss(params, first_sums, targets):
    w_second, b_second, norm_gain, norm_shift = params
    hidden = first_sums * jax.nn.sigmoid(first_sums)
    zsecond = (
        jnp.dot(hidden, w_second, precision=prec, preferred_element_type=jnp.float32) + b_second
    )
    center = zsecond - jnp.mean(zsecond, axis=1, keepdims=True)
    spread = jnp.mean(center * center, axis=1, keepdims=True)
    output = center * lax.rsqrt(spread + 1e-05) * norm_gain + norm_shift
    return 0.5 * jnp.sum((output - targets) ** 2) / first_sums.shape[0]


class Sizes:
    def __init__(self, n_ada, n_avg, width):
        self.n_ada, self.n_avg, self.width = n_ada, n_avg, width
        self.core = 2 if n_ada % 2 == 0 else 1
        self.y = n_ada // self.core
        self.x = self.y if n_avg % self.y == 0 else 1
        self.z = n_avg // self.x
        self.cols = width // self.x
        self.stat_rows = -(-(n_ada * (n_ada + 1) // 2) // 8) * 8

    def tensor_copies(self):
        gather = 2 * (self.z - 1) + self.x - 1 + 2 * (self.y - 1) + self.y * (self.x - 1)
        gather += 2 * self.y * (self.core - 1)
        scatter = 2 * (self.x - 1) + 2 * (self.z - 1)
        return 2 * (self.n_ada - 1) + scatter + gather

    def copies(self):
        return 2 * self.tensor_copies() + self.n_ada - 1 + self.n_avg - 1


def chunk_of(rows):
    return next(c for c in (32, 16, 8) if rows % c == 0)


def over_chunks(rows, body, init=0, size=None):
    size = size or chunk_of(rows)

    def step(i, carry):
        return body(pl.ds(pl.multiple_of(i * size, size), size), carry)

    return lax.fori_loop(0, rows // size, step, init)


def folded(block):
    return jnp.sum(block.reshape(block.shape[0] // 8, 8, block.shape[1]), axis=0)


def split(value):
    high = value.astype(jnp.bfloat16)
    return high, (value - high.astype(jnp.float32)).astype(jnp.bfloat16)


def contracted(left, right):
    return lax.dot_general(
        left, right, (((0,), (0,)), ((), ())), preferred_element_type=jnp.float32
    )


def coefficients(dot, norm_a, norm_b):
    return (
        1.0 - dot / (2.0 * (norm_a + norm_eps)),
        1.0 - dot / (2.0 * (norm_b + norm_eps)),
    )


def adasum_weights(inner, count):
    def product(i, j):
        return inner[min(i, j), max(i, j)]

    weights = [{a: jnp.ones((1, 1), jnp.float32)} for a in range(count)]
    while count > 1:
        half = count // 2
        coefs = [
            coefficients(product(p, p + half), product(p, p), product(p + half, p + half))
            for p in range(half)
        ]
        merged, following = [], {}
        for p in range(half):
            both = {a: coefs[p][0] * w for a, w in weights[p].items()}
            both.update({a: coefs[p][1] * w for a, w in weights[p + half].items()})
            merged.append(both)
            for q in range(p, half):
                value = 0.0
                for i, left in zip((p, p + half), coefs[p]):
                    for j, right in zip((q, q + half), coefs[q]):
                        value = value + left * right * product(i, j)
                following[p, q] = jnp.maximum(value, 0.0) if p == q else value
        weights, inner, count = merged, following, half
    return [weights[0][a] for a in sorted(weights[0])]


def comm_kernel(sz, *refs):
    x_ref, dz_ref, g_second, g_vec, out_first, out_second, out_vec = refs[:7]
    scratch = refs[7:]
    per_first, per_second = scratch[:8], scratch[8:16]
    vec_ada, vec_avg, send, recv, local_sem = scratch[16:21]
    g_first, x_buf, dz_high, dz_low, x_sem = scratch[21:]

    me, v = lax.axis_index("ada"), lax.axis_index("avg")
    y, core = me // sz.core, me % sz.core
    z, x = v // sz.x, v % sz.x

    def ada_peer(a):
        return {"ada": a, "avg": v}

    def avg_peer(b):
        return {"ada": me, "avg": b}

    sub = x_buf.shape[2]
    chunk = x_ref.shape[1] // sz.y
    firsts = [
        jnp.bitwise_xor(y, k) * chunk + i * sub
        for k in list(range(1, sz.y)) + [0]
        for i in range(chunk // sub)
    ]
    loads = [
        pltpu.make_async_copy(
            x_ref.at[:, pl.ds(pl.multiple_of(first, 128), sub)],
            x_buf.at[i % 2], x_sem.at[i % 2],
        )
        for i, first in enumerate(firsts)
    ]
    for load in loads[:2]:
        load.start()

    def weight_grad(i):
        loads[i].wait()
        high, low = split(x_buf[i % 2])
        if i + 2 < len(loads):
            loads[i + 2].start()
        value = contracted(high, dz_low[...]) + contracted(low, dz_high[...])
        rows = pl.ds(pl.multiple_of(firsts[i], 8), sub)
        g_first[rows] = value + contracted(high, dz_high[...])

    barrier = pltpu.get_barrier_semaphore()
    peers = [ada_peer(lax.rem(me + k, sz.n_ada)) for k in range(1, sz.n_ada)]
    peers += [avg_peer(lax.rem(v + k, sz.n_avg)) for k in range(1, sz.n_avg)]
    for peer in peers:
        pl.semaphore_signal(barrier, inc=1, device_id=peer, device_id_type=pl.DeviceIdType.MESH)
    pl.semaphore_wait(barrier, len(peers))

    started = []

    def start(src, dst, peer):
        i = len(started)
        copy = pltpu.make_async_remote_copy(
            src_ref=src, dst_ref=dst, send_sem=send.at[i], recv_sem=recv.at[i],
            device_id=peer, device_id_type=pl.DeviceIdType.MESH,
        )
        copy.start()
        started.append(copy)
        return copy

    def arrived(copies):
        for copy in copies:
            copy.wait_recv()

    vec_copies = []
    for k in range(1, sz.n_ada):
        peer = lax.rem(me + k, sz.n_ada)
        vec_copies.append(start(g_vec, vec_ada.at[me], ada_peer(peer)))
    sides = ((g_second, per_second), (g_first, per_first))
    own_copies = []
    slices = ([], [])
    for t, (grad, per) in enumerate(sides):
        part = grad.shape[0] // sz.n_ada
        rows = pl.ds(pl.multiple_of(me * part, 8), part)
        own_copies.append(
            pltpu.make_async_copy(grad.at[rows], per[0].at[me], local_sem.at[t])
        )
    own_copies[0].start()

    def give(t, offsets):
        grad, per = sides[t]
        part = grad.shape[0] // sz.n_ada
        for k in offsets:
            peer = jnp.bitwise_xor(me, k)
            rows = pl.ds(pl.multiple_of(peer * part, 8), part)
            slices[t].append(start(grad.at[rows], per[0].at[me], ada_peer(peer)))

    far, near = list(range(sz.core, sz.n_ada)), list(range(1, sz.core))
    cut = len(far) // 2
    give(0, far + near)

    def split_rows(rows, carry):
        dz_high[rows], dz_low[rows] = split(dz_ref[rows])
        return carry

    over_chunks(dz_ref.shape[0], split_rows)
    away = len(loads) - chunk // sub
    for i in range(away):
        weight_grad(i)
    give(1, far[:cut])
    for i in range(away, len(loads)):
        weight_grad(i)
    give(1, near)
    own_copies[1].start()

    vec_ada[me] = g_vec[...]
    arrived(vec_copies)
    items = [vec_ada[a] for a in range(sz.n_ada)]
    while len(items) > 1:
        half = len(items) // 2
        merged = []
        for a, b in zip(items[:half], items[half:]):
            dot = jnp.sum(a * b, axis=1, keepdims=True)
            norm_a = jnp.sum(a * a, axis=1, keepdims=True)
            norm_b = jnp.sum(b * b, axis=1, keepdims=True)
            coef_a, coef_b = coefficients(dot, norm_a, norm_b)
            merged.append(coef_a * a + coef_b * b)
        items = merged
    vec_avg[v] = items[0]
    vec_out = []
    for k in range(1, sz.n_avg):
        peer = lax.rem(v + k, sz.n_avg)
        vec_out.append(start(vec_avg.at[v], vec_avg.at[v], avg_peer(peer)))

    def tensor(t, grad, out, per):
        got, stats, x_a, sum_a, z_a, z_b, sum_b, x_b = per
        part = grad.shape[0] // sz.n_ada
        strip = part // 2
        piece = strip // sz.z
        cols = sz.cols
        own_copies[t].wait()
        arrived(slices[t])

        pairs = [(i, j) for i in range(sz.n_ada) for j in range(i, sz.n_ada)]
        mine = stats.at[me]
        mine[...] = jnp.zeros((sz.stat_rows, sz.width), jnp.float32)
        for some in (pairs[i : i + 5] for i in range(0, len(pairs), 5)):

            def add(rows, carry):
                used = {i: got[i, rows] for pair in some for i in pair}
                return tuple(c + folded(used[i] * used[j]) for c, (i, j) in zip(carry, some))

            zero = jnp.zeros((8, sz.width), jnp.float32)
            sums = over_chunks(part, add, (zero,) * len(some), 8)
            for pair, value in zip(some, sums):
                row = pairs.index(pair)
                mine[row : row + 1, :] = jnp.sum(value, axis=0, keepdims=True)
        stat_copies = []
        for k in range(1, sz.n_ada):
            peer = lax.rem(me + k, sz.n_ada)
            stat_copies.append(start(stats.at[me], stats.at[me], ada_peer(peer)))
        yield
        arrived(stat_copies)
        gathered = stats[0]
        for a in range(1, sz.n_ada):
            gathered = gathered + stats[a]
        gathered = jnp.sum(gathered, axis=1, keepdims=True)
        weights = adasum_weights(
            {pair: gathered[row : row + 1] for row, pair in enumerate(pairs)}, sz.n_ada
        )

        def merge(rows, carry):
            value = weights[0] * got[0, rows]
            for a in range(1, sz.n_ada):
                value = value + weights[a] * got[a, rows]
            got[0, rows] = value
            return carry

        over_chunks(part, merge)

        def at_x(i):
            return pl.ds(pl.multiple_of(i * cols, 128), cols)

        def at_z(i, base=0):
            return pl.ds(pl.multiple_of(base + i * piece, 8), piece)

        def z_peer(k):
            return lax.rem(z + k, sz.z)

        def x_peer(k):
            return lax.rem(x + k, sz.x)

        def z_dev(i):
            return avg_peer(i * sz.x + x)

        def x_dev(i):
            return avg_peer(z * sz.x + i)

        def total(rows, read, buffer, write):
            def body(window, carry):
                value = read(window)
                for k in range(buffer.shape[0]):
                    value = value + buffer[k, window]
                write(window, value)
                return carry

            over_chunks(rows, body)

        def shifted(window, base):
            return pl.ds(pl.multiple_of(base + window.start, 8), window.size)

        whole = got.at[0]
        a_x = [
            start(whole.at[pl.ds(0, strip), at_x(x_peer(k))], x_a.at[k - 1], x_dev(x_peer(k)))
            for k in range(1, sz.x)
        ]
        b_z = [
            start(whole.at[at_z(z_peer(k), strip)], z_b.at[k - 1], z_dev(z_peer(k)))
            for k in range(1, sz.z)
        ]

        def put(ref):
            def write(window, value):
                ref[window] = value

            return write

        def put_out(base):
            def write(window, value):
                out[shifted(window, base), at_x(x)] = value

            return write

        yield
        arrived(a_x)
        total(strip, lambda w: got[0, w, at_x(x)], x_a, put(sum_a))
        a_z = [
            start(sum_a.at[at_z(z_peer(k))], z_a.at[k - 1], z_dev(z_peer(k)))
            for k in range(1, sz.z)
        ]
        yield
        arrived(b_z)
        total(piece, lambda w: got[0, shifted(w, strip + z * piece)], z_b, put(sum_b))
        b_x = [
            start(sum_b.at[:, at_x(x_peer(k))], x_b.at[k - 1], x_dev(x_peer(k)))
            for k in range(1, sz.x)
        ]

        def base_of(side, row_y):
            return (row_y * sz.core + core) * part + side * strip

        def spread(side, row_y, columns, peer):
            rows = pl.ds(pl.multiple_of(base_of(side, row_y), 8), strip)
            block = out.at[rows] if columns is None else out.at[rows, columns]
            return start(block, block, peer)

        def spread_z(side):
            block = out.at[at_z(z, base_of(side, y)), at_x(x)]
            return [start(block, block, z_dev(z_peer(k))) for k in range(1, sz.z)]

        def y_row(k):
            return lax.rem(y + k, sz.y)

        def spread_y(side, columns):
            return [
                spread(side, y, columns, ada_peer(y_row(k) * sz.core + core))
                for k in range(1, sz.y)
            ]

        def spread_x(side, row_y):
            return [spread(side, row_y, at_x(x), x_dev(x_peer(k))) for k in range(1, sz.x)]

        def spread_core(side, row_y):
            return [
                spread(side, row_y, None, ada_peer(y * sz.core + lax.rem(core + k, sz.core)))
                for k in range(1, sz.core)
            ]

        yield
        arrived(a_z)
        total(piece, lambda w: sum_a[shifted(w, z * piece)], z_a, put_out(base_of(0, y) + z * piece))
        a_gather = spread_z(0)
        yield
        arrived(b_x)
        total(piece, lambda w: sum_b[w, at_x(x)], x_b, put_out(base_of(1, y) + z * piece))
        b_gather = spread_z(1)

        yield
        arrived(a_gather)
        a_x = spread_x(0, y)
        yield
        arrived(b_gather)
        b_y = spread_y(1, at_x(x))
        b_x = spread_x(1, y)
        yield
        arrived(a_x)
        a_y = spread_y(0, None)
        last = spread_core(0, y)
        yield
        arrived(b_y)
        b_x_far = []
        for k in range(1, sz.y):
            b_x_far += spread_x(1, y_row(k))
        yield
        arrived(b_x)
        last += spread_core(1, y)
        yield
        arrived(a_y)
        for k in range(1, sz.y):
            last += spread_core(0, y_row(k))
        yield
        arrived(b_x_far)
        for k in range(1, sz.y):
            last += spread_core(1, y_row(k))
        yield
        arrived(last)

    second = tensor(0, g_second, out_second, per_second)
    first = tensor(1, g_first, out_first, per_first)
    next(second)
    give(1, far[cut:])
    for _ in range(8):
        next(second)
    arrived(vec_out)
    vec_total = vec_avg[0]
    for b in range(1, sz.n_avg):
        vec_total = vec_total + vec_avg[b]
    out_vec[...] = vec_total
    running = [first, second]
    while running:
        running = [one for one in running if next(one, True) is None]

    for copy in started:
        copy.wait_send()


def tensor_scratch(sz, rows):
    part = rows // sz.n_ada
    strip = part // 2
    piece = strip // sz.z

    def vmem(*shape):
        return pltpu.VMEM(shape, jnp.float32)

    return [
        vmem(sz.n_ada, part, sz.width),
        vmem(sz.n_ada, sz.stat_rows, sz.width),
        vmem(max(sz.x - 1, 1), strip, sz.cols),
        vmem(strip, sz.cols),
        vmem(max(sz.z - 1, 1), piece, sz.cols),
        vmem(max(sz.z - 1, 1), piece, sz.width),
        vmem(piece, sz.width),
        vmem(max(sz.x - 1, 1), piece, sz.cols),
    ]


def adasum_totals(edges, delta, second, vectors):
    sz = Sizes(lax.axis_size("ada"), lax.axis_size("avg"), delta.shape[1])
    rows, d_in = edges.shape
    chunk = d_in // sz.y
    sub = next(c for c in (384, 256, 128) if chunk % c == 0)
    first = jax.ShapeDtypeStruct((d_in, delta.shape[1]), jnp.float32)
    in_vmem = pl.BlockSpec(memory_space=pltpu.VMEM)
    anywhere = pl.BlockSpec(memory_space=pl.ANY)
    return pl.pallas_call(
        functools.partial(comm_kernel, sz),
        out_shape=[jax.ShapeDtypeStruct(a.shape, a.dtype) for a in (first, second, vectors)],
        in_specs=[anywhere, in_vmem, anywhere, in_vmem],
        out_specs=[in_vmem] * 3,
        scratch_shapes=tensor_scratch(sz, first.shape[0])
        + tensor_scratch(sz, second.shape[0])
        + [
            pltpu.VMEM((sz.n_ada,) + vectors.shape, jnp.float32),
            pltpu.VMEM((sz.n_avg,) + vectors.shape, jnp.float32),
            pltpu.SemaphoreType.DMA((sz.copies(),)),
            pltpu.SemaphoreType.DMA((sz.copies(),)),
            pltpu.SemaphoreType.DMA((2,)),
            pltpu.VMEM(first.shape, jnp.float32),
            pltpu.VMEM((2, rows, sub), jnp.float32),
            pltpu.VMEM(delta.shape, jnp.bfloat16),
            pltpu.VMEM(delta.shape, jnp.bfloat16),
            pltpu.SemaphoreType.DMA((2,)),
        ],
        compiler_params=pltpu.CompilerParams(
            collective_id=0, has_side_effects=True, vmem_limit_bytes=40 * 2**20
        ),
        name="adasum_totals",
    )(edges, delta, second, vectors)


def local(edges, teacher, w_first, b_first, w_second, b_second, norm_gain, norm_shift):
    first_sums = (
        jnp.dot(edges, w_first, precision=prec, preferred_element_type=jnp.float32) + b_first
    )
    params = (w_second, b_second, norm_gain, norm_shift)
    grads, delta = jax.grad(local_loss, argnums=(0, 1))(params, first_sums, teacher)
    vectors = jnp.stack([jnp.sum(delta, axis=0), grads[1], grads[2], grads[3]])
    vectors = jnp.concatenate([vectors, jnp.zeros_like(vectors)], axis=0)
    first, second, vec = adasum_totals(edges, delta, grads[0], vectors)
    avg_count = lax.axis_size("avg")

    def new(param, total):
        return param - step_rate * (total / avg_count)

    return (
        new(w_first, first),
        new(b_first, vec[0]),
        new(w_second, second),
        new(b_second, vec[1]),
        new(norm_gain, vec[2]),
        new(norm_shift, vec[3]),
    )


def solution(mesh):
    in_specs = (P(("ada", "avg"), None), P(("ada", "avg"), None), P(), P(), P(), P(), P(), P())
    out_specs = (P(), P(), P(), P(), P(), P())
    return jax.shard_map(local, mesh=mesh, in_specs=in_specs, out_specs=out_specs, check_vma=False)
```
